32 devices in a mesh: groups: 2 (over x), ctx: 16 (over z, y, core).
Axes of the slice: x: 2, y: 2, z: 4, core: 2. Of those that a mesh axis runs over, the one named last changes fastest.
Arguments:
- rotated_queries: bfloat16 [4096, 2048], P(('groups', 'ctx')), parts along dimension 0, may hold values from -6.5 to 6.5
- key_rows: bfloat16 [4096, 512], P(('groups', 'ctx')), parts along dimension 0, may hold values from -6.5 to 6.5
- value_matrix: bfloat16 [4096, 512], P(('groups', 'ctx')), parts along dimension 0, may hold values from -6 to 6
- doc_lengths: int32 [8], P('groups'), parts along dimension 0, may hold values from 1 to 1024, 2048 in all
Outputs:
- attended: bfloat16 [4096, 2048], P(('groups', 'ctx')), parts along dimension 0
The draws below stay inside these ranges and needn't reach their ends.
There are 2 independent parts, one for each index of `groups`. The reference program is written for one: setup_inputs(seed, part) draws one part's arguments, and reference() takes and returns one part's arrays. A program takes and returns all parts, laid end to end along the dimension named above; each array names one. Nothing has to cross between parts.
Inputs may be any that keep to these rules, and one draw needn't show every extreme that they name: `doc_lengths`: the 4 lengths of one part sum to 2048; the largest is exactly 1024.
All inputs are finite; a program needn't handle non-finite values.
Results may differ from the reference program's by a relative error of at most 0.005.
Values may be sent and summed in bfloat16 or wider, within the bound.
No kernel may reach another device: no remote copies, remote signals or barrier semaphores. Data moves between devices by JAX's collectives and lax.ppermute only.
A program may use at most 128 MiB of HBM per device.

```python
import math
import jax
import jax.numpy as jnp
import numpy as np
from jax import lax

QUERY_HEADS = 16
KEY_VALUE_HEADS = 4
HEAD_WIDTH = 128
TOKENS_PER_SHARD = 128
DOCS = 4
LONGEST_LENGTH = 1024
CONTEXT_TOKENS = 2048


def starting_rows(key, width):
    normal_part = jnp.clip(jax.random.normal(key, (CONTEXT_TOKENS, width), jnp.float32), -4.0, 4.0)
    return normal_part


def draw_rotated_queries(key, part):
    output_values = starting_rows(jax.random.fold_in(key, 1), QUERY_HEADS * HEAD_WIDTH)
    return output_values.astype(jnp.bfloat16)


def draw_key_rows(key, part):
    output_values = starting_rows(jax.random.fold_in(key, 2), KEY_VALUE_HEADS * HEAD_WIDTH)
    return output_values.astype(jnp.bfloat16)


def steps_of(own_key, shape, pieces, smallest, high):
    loudness = 1.0
    for dim, shards_of in pieces:
        draws = jax.random.uniform(jax.random.fold_in(jax.random.fold_in(own_key, 6), dim), (shards_of,), jnp.float32, smallest / len(pieces), high / len(pieces))
        loudness = loudness * jnp.repeat(jnp.exp(draws), shape[dim] // shards_of).reshape((-1,) + (1,) * (len(shape) - 1 - dim))
    return loudness


def profile(amount, total, most, slope):
    weights = [(1 << 20) // math.isqrt(standing ** slope) + 1 for standing in range(2, amount + 1)]
    surplus, counts = total - most - (amount - 1), [1] * (amount - 1)
    while surplus > 0:
        free = [i for i in range(amount - 1) if counts[i] < most]
        whole, budget = sum([weights[i] for i in free]), surplus
        for i in free:
            addition = min(most - counts[i], max(1, budget * weights[i] // whole), surplus)
            counts[i] = counts[i] + addition
            surplus = surplus - addition
    return np.array([most] + counts)


def ragged(stream_key, count, total, limit, skew):
    if count == 2:
        one = jax.random.randint(stream_key, (), max(1, total - limit), min(limit, total - 1) + 1)
        return jnp.stack([one, total - one])
    sizes = jnp.asarray(profile(count, total, limit, skew), jnp.int32)
    twos = (count - 1) // 2
    source_of, receiver = sizes[1:1 + 2 * twos:2], sizes[2:2 + 2 * twos:2]
    margin = jnp.minimum(source_of - 1, limit - receiver)
    passed = jax.random.randint(jax.random.fold_in(stream_key, 1), (twos,), 0, 1 << 20) % (margin + 1)
    sizes = sizes.at[1:1 + 2 * twos:2].set(source_of - passed).at[2:2 + 2 * twos:2].set(receiver + passed)
    return sizes[jax.random.permutation(jax.random.fold_in(stream_key, 2), count)]


def gaussian(key, extent, scale, most, cuts=(), kind=jnp.bfloat16):
    result = jax.random.normal(key, extent, jnp.float32) * scale
    if len(cuts) > 0:
        result = steps_of(key, extent, cuts, -0.22, 0.18) * result
    return jnp.clip(result, min=-most, max=most).astype(kind)


def setup_inputs(seed: int = 0, part: int = 0) -> dict:
    seeds = jax.random.split(jax.random.key(seed), 5)
    part_keys = jax.random.split(jax.random.fold_in(seeds[4], part), 5)
    return {
        "rotated_queries": draw_rotated_queries(jax.random.fold_in(jax.random.fold_in(seeds[4], part), 71), part),
        "key_rows": draw_key_rows(jax.random.fold_in(jax.random.fold_in(seeds[4], part), 71), part),
        "value_matrix": gaussian(part_keys[2], (CONTEXT_TOKENS, KEY_VALUE_HEADS * HEAD_WIDTH), 1.0, 6.0, ((0, 16),)),
        "doc_lengths": ragged(part_keys[3], DOCS, CONTEXT_TOKENS, LONGEST_LENGTH, 2).astype(jnp.int32),
    }


def reference(rotated_queries, key_rows, value_matrix, doc_lengths):
    group_width = QUERY_HEADS // KEY_VALUE_HEADS
    positions = jnp.arange(CONTEXT_TOKENS, dtype=jnp.int32)
    doc_ends = jnp.cumsum(doc_lengths).astype(jnp.int32)
    starts_all = jnp.sum(jnp.where(doc_ends[None, :] <= positions[:, None], doc_lengths[None, :], 0), axis=1).astype(jnp.int32)
    padding_rows = jnp.zeros((LONGEST_LENGTH, KEY_VALUE_HEADS * HEAD_WIDTH), jnp.bfloat16)
    padded_keys = jnp.concatenate([padding_rows, key_rows], axis=0)
    padded_values = jnp.concatenate([padding_rows, value_matrix], axis=0)
    visible_window = LONGEST_LENGTH + TOKENS_PER_SHARD

    def one_block(block_number):
        first_index = (block_number * TOKENS_PER_SHARD).astype(jnp.int32)
        query_tile_rows = lax.dynamic_slice_in_dim(rotated_queries, first_index, TOKENS_PER_SHARD, 0).astype(jnp.float32).reshape(TOKENS_PER_SHARD, KEY_VALUE_HEADS, group_width, HEAD_WIDTH)
        key_tile_rows = lax.dynamic_slice_in_dim(padded_keys, first_index, visible_window, 0).astype(jnp.float32).reshape(visible_window, KEY_VALUE_HEADS, HEAD_WIDTH)
        value_tile_rows = lax.dynamic_slice_in_dim(padded_values, first_index, visible_window, 0).astype(jnp.float32).reshape(visible_window, KEY_VALUE_HEADS, HEAD_WIDTH)
        query_pos = first_index + jnp.arange(TOKENS_PER_SHARD, dtype=jnp.int32)
        query_start = lax.dynamic_slice_in_dim(starts_all, first_index, TOKENS_PER_SHARD, 0)
        key_pos = first_index - LONGEST_LENGTH + jnp.arange(visible_window, dtype=jnp.int32)
        scores = jnp.einsum("tkgd,skd->tkgs", query_tile_rows, key_tile_rows) * (HEAD_WIDTH ** -0.5)
        allowed = (key_pos[None, :] >= query_start[:, None]) & (key_pos[None, :] <= query_pos[:, None])
        allowed = allowed[:, None, None, :]
        scores = jnp.where(allowed, scores, jnp.float32(-1e30))
        row_max = jnp.max(scores, axis=-1, keepdims=True)
        weights = jnp.where(allowed, jnp.exp(scores - row_max), jnp.float32(0.0))
        total = jnp.sum(weights, axis=-1)
        weight_half = lax.optimization_barrier(weights.astype(jnp.bfloat16)).astype(jnp.float32)
        mixed = jnp.einsum("tkgs,skd->tkgd", weight_half, value_tile_rows) / total[..., None]
        return mixed.astype(jnp.bfloat16).reshape(TOKENS_PER_SHARD, QUERY_HEADS * HEAD_WIDTH)

    blocks = lax.map(one_block, jnp.arange(CONTEXT_TOKENS // TOKENS_PER_SHARD, dtype=jnp.int32))
    return blocks.reshape(CONTEXT_TOKENS, QUERY_HEADS * HEAD_WIDTH)
```

```python
import functools
import math

import jax
import jax.numpy as jnp
from jax import lax
from jax.experimental import pallas as pl
from jax.experimental.pallas import tpu as pltpu
from jax.sharding import PartitionSpec as P

QUERY_HEADS = 16
KEY_VALUE_HEADS = 4
HEAD_WIDTH = 128
GROUP = QUERY_HEADS // KEY_VALUE_HEADS

masked_score = -1e30
LOG2_SCALE = math.log2(math.e) * HEAD_WIDTH ** (-0.5)


def from_behind(shard, axis, by):
    peers = lax.axis_size(axis)
    pairs = [(i, i + by) for i in range(peers) if 0 <= i + by < peers]
    return lax.ppermute(shard, axis, pairs)


def doc_start_of(query_pos, doc_lengths):
    doc_ends = jnp.cumsum(doc_lengths)
    taken_lengths = jnp.where(doc_ends[None, :] <= query_pos[:, None], doc_lengths[None, :], 0)
    return jnp.sum(taken_lengths, axis=1)


def fold_block(state_now, block_slice, key_start, grouped_heads, query_pos, query_start):
    run_max, run_sum, accumulated = state_now
    token_count = block_slice.shape[1]
    local_keys = block_slice[0].reshape(token_count, KEY_VALUE_HEADS, HEAD_WIDTH)
    local_values = block_slice[1].reshape(token_count, KEY_VALUE_HEADS, HEAD_WIDTH)
    scores = jnp.einsum(
        "tkgd,skd->tkgs", grouped_heads, local_keys, preferred_element_type=jnp.float32
    ) * HEAD_WIDTH ** (-0.5)
    key_pos = key_start + jnp.arange(token_count, dtype=jnp.int32)
    allowed = (key_pos[None, :] >= query_start[:, None]) & (key_pos[None, :] <= query_pos[:, None])
    allowed = allowed[:, None, None, :]
    scores = jnp.where(allowed, scores, masked_score)
    new_max = jnp.maximum(run_max, jnp.max(scores, axis=-1))
    weights = jnp.where(allowed, jnp.exp(scores - new_max[..., None]), 0.0)
    factor = jnp.exp(run_max - new_max)
    run_sum = run_sum * factor + jnp.sum(weights, axis=-1)
    accumulated = accumulated * factor[..., None] + jnp.einsum(
        "tkgs,skd->tkgd",
        weights.astype(jnp.bfloat16),
        local_values,
        preferred_element_type=jnp.float32,
    )
    return (new_max, run_sum, accumulated)


def general_device(rotated_queries, key_rows, value_matrix, doc_lengths):
    count_of_rows = rotated_queries.shape[0]
    span_count = lax.axis_size("ctx") // 2
    device_index = lax.axis_index("ctx")
    query_pos = device_index * count_of_rows + jnp.arange(count_of_rows, dtype=jnp.int32)
    query_start = doc_start_of(query_pos, doc_lengths)
    grouped_heads = rotated_queries.reshape(count_of_rows, KEY_VALUE_HEADS, GROUP, HEAD_WIDTH)
    statistic_shape = (count_of_rows, KEY_VALUE_HEADS, GROUP)
    state_now = (
        jnp.full(statistic_shape, masked_score, jnp.float32),
        jnp.zeros(statistic_shape, jnp.float32),
        jnp.zeros(statistic_shape + (HEAD_WIDTH,), jnp.float32),
    )
    own_block = jnp.stack([key_rows, value_matrix])
    state_now = fold_block(
        state_now, own_block, device_index * count_of_rows, grouped_heads, query_pos, query_start
    )
    stored = own_block[None]
    for level_number in range(16):
        held_count = stored.shape[0]
        send_count = min(held_count, span_count + 1 - held_count)
        if send_count > 0:
            arrived = from_behind(stored[:send_count], "ctx", held_count)

            def arrived_step(offset_number, inner_state, arrived=arrived, held_count=held_count):
                block_slice = lax.dynamic_index_in_dim(arrived, offset_number, 0, keepdims=False)
                key_start = (device_index - held_count - offset_number) * count_of_rows
                return fold_block(
                    inner_state, block_slice, key_start, grouped_heads, query_pos, query_start
                )

            state_now = lax.fori_loop(0, send_count, arrived_step, state_now)
            stored = jnp.concatenate([stored, arrived], axis=0)
    run_max, run_sum, accumulated = state_now
    result = accumulated / run_sum[..., None]
    return result.reshape(count_of_rows, QUERY_HEADS * HEAD_WIDTH).astype(jnp.bfloat16)


WIDE = 512
VMEM_BYTES = 16 << 20


def attend_body(origins, docs, first, last, *refs):
    count = len(origins)
    refs = list(refs)
    lengths_ref, query_ref = refs[0], refs[1]
    key_refs, value_refs = refs[2 : 2 + count], refs[2 + count : 2 + 2 * count]
    rest = refs[2 + 2 * count :]
    if not first:
        max_in, sum_in, acc_in = rest[:3]
        rest = rest[3:]
    if last:
        out_ref, bias_ref = rest
    else:
        max_out, sum_out, acc_out, bias_ref = rest
    rows = query_ref.shape[0]
    me = lax.axis_index("ctx")
    peers = lax.axis_size("ctx")
    query_pos = me * rows + lax.broadcasted_iota(jnp.int32, (1, rows), 1)
    query_start = jnp.zeros((1, rows), jnp.int32)
    end = jnp.int32(0)
    for j in range(docs):
        end = end + lengths_ref[j]
        query_start = query_start + jnp.where(end <= query_pos, lengths_ref[j], 0)
    for i, (back, flip) in enumerate(origins):
        origin = lax.rem(me + (peers - back), peers) ^ flip
        key_pos = origin * rows + lax.broadcasted_iota(jnp.int32, (rows, rows), 0)
        allowed = (key_pos >= query_start) & (key_pos <= query_pos)
        bias_ref[i] = jnp.where(allowed, 0.0, masked_score)
    per = WIDE // rows
    for head in range(0, QUERY_HEADS, per):
        kv = slice(head // GROUP * HEAD_WIDTH, (head // GROUP + 1) * HEAD_WIDTH)
        columns = slice(head * rows, (head + per) * rows)
        stacked = jnp.concatenate(
            [query_ref[:, h * HEAD_WIDTH : (h + 1) * HEAD_WIDTH] for h in range(head, head + per)],
            axis=0,
        )
        scores = []
        for i in range(count):
            raw = lax.dot_general(
                key_refs[i][:, kv],
                stacked,
                (((1,), (1,)), ((), ())),
                preferred_element_type=jnp.float32,
            )
            scores.append(raw * LOG2_SCALE + jnp.concatenate([bias_ref[i]] * per, axis=1))
        top = functools.reduce(jnp.maximum, scores)
        new_max = jnp.max(top, axis=0, keepdims=True)
        if not first:
            old_max = max_in[0:1, columns]
            new_max = jnp.maximum(new_max, old_max)
            factor = jnp.exp2(old_max - new_max)
        weights = [jnp.exp2(s - new_max) for s in scores]
        new_sum = jnp.sum(functools.reduce(jnp.add, weights), axis=0, keepdims=True)
        half = jnp.concatenate([w.astype(jnp.bfloat16) for w in weights], axis=0)
        values = jnp.concatenate([v[:, kv] for v in value_refs], axis=0)
        mixed = lax.dot_general(
            values, half, (((0,), (0,)), ((), ())), preferred_element_type=jnp.float32
        )
        if not first:
            new_sum = new_sum + factor * sum_in[0:1, columns]
            mixed = mixed + factor * acc_in[:, columns]
        if last:
            mixed = mixed * (1.0 / new_sum)
            for j in range(per):
                piece = mixed[:, j * rows : (j + 1) * rows].T.astype(jnp.bfloat16)
                out_ref[:, (head + j) * HEAD_WIDTH : (head + j + 1) * HEAD_WIDTH] = piece
        else:
            max_out[0:1, columns] = new_max
            sum_out[0:1, columns] = new_sum
            acc_out[:, columns] = mixed


def attend(lengths, queries, blocks, state=None, last=False, name=None):
    origins = tuple(origin for origin, _, _ in blocks)
    keys = [k for _, k, _ in blocks]
    values = [v for _, _, v in blocks]
    rows = queries.shape[0]
    stats = jax.ShapeDtypeStruct((1, QUERY_HEADS * rows), jnp.float32)
    acc = jax.ShapeDtypeStruct((HEAD_WIDTH, QUERY_HEADS * rows), jnp.float32)
    vmem = pl.BlockSpec(memory_space=pltpu.VMEM)
    operands = [lengths, queries, *keys, *values, *(state or ())]
    if last:
        out_shape, out_specs = jax.ShapeDtypeStruct(queries.shape, jnp.bfloat16), vmem
    else:
        out_shape, out_specs = (stats, stats, acc), (vmem, vmem, vmem)
    return pl.pallas_call(
        functools.partial(attend_body, origins, lengths.shape[0], state is None, last),
        out_shape=out_shape,
        in_specs=[pl.BlockSpec(memory_space=pltpu.SMEM)] + [vmem] * (len(operands) - 1),
        out_specs=out_specs,
        scratch_shapes=[pltpu.VMEM((len(blocks), rows, rows), jnp.float32)],
        name=name,
        compiler_params=pltpu.CompilerParams(vmem_limit_bytes=VMEM_BYTES),
        cost_estimate=pl.CostEstimate(
            flops=4 * rows * rows * QUERY_HEADS * HEAD_WIDTH * len(blocks),
            transcendentals=rows * rows * QUERY_HEADS * len(blocks),
            bytes_accessed=2 * rows * KEY_VALUE_HEADS * HEAD_WIDTH * 2 * len(blocks),
        ),
    )(*operands)


def plane_device(rotated_queries, key_rows, value_matrix, doc_lengths):
    peers = lax.axis_size("ctx")
    planes = [(i, (i + 4) % peers) for i in range(peers)]
    chips = [(i, i ^ 2) for i in range(peers)]
    cores = [(i, i ^ 1) for i in range(peers)]

    def move(pair, pairs):
        return tuple(lax.ppermute(a, "ctx", pairs) for a in pair)

    own = (key_rows, value_matrix)
    below = move(own, planes)
    own_core = move(own, cores)
    own_chip = move(own, chips)
    own_both = move(own_chip, cores)
    below_chip = move(below, chips)
    below_core = move(below, cores)
    below_both = move(below_chip, cores)
    deep = move(below, planes)
    deep_core = move(deep, cores)
    deep_chip = move(deep, chips)
    deep_both = move(deep_chip, cores)

    def block(back, flip, pair):
        return ((back, flip), *pair)

    state = attend(
        doc_lengths,
        rotated_queries,
        [block(0, 0, own), block(0, 1, own_core), block(0, 2, own_chip), block(0, 3, own_both)],
        name="own_plane",
    )
    state = attend(
        doc_lengths,
        rotated_queries,
        [
            block(4, 0, below),
            block(4, 1, below_core),
            block(4, 2, below_chip),
            block(4, 3, below_both),
        ],
        state,
        name="plane_below",
    )
    state = attend(
        doc_lengths,
        rotated_queries,
        [block(8, 0, deep), block(8, 1, deep_core)],
        state,
        name="deep_own_chip",
    )
    return attend(
        doc_lengths,
        rotated_queries,
        [block(8, 2, deep_chip), block(8, 3, deep_both)],
        state,
        last=True,
        name="deep_other_chip",
    )


def solution(mesh):
    in_specs = (
        P(("groups", "ctx"), None),
        P(("groups", "ctx"), None),
        P(("groups", "ctx"), None),
        P("groups"),
    )
    out_specs = P(("groups", "ctx"), None)
    per_device = plane_device if mesh.shape["ctx"] == 16 else general_device
    return jax.shard_map(
        per_device, mesh=mesh, in_specs=in_specs, out_specs=out_specs, check_vma=False
    )
```
